32 devices in a mesh: dp: 8 (over z, y), feat: 4 (over x, core).
Axes of the slice: x: 2, y: 2, z: 4, core: 2. Of those that a mesh axis runs over, the one named last changes fastest.
Arguments:
- observations: bfloat16 [1024, 128, 128], P('dp', 'feat'), may hold values from -1.5 to 1.5
- labels: int32 [1024, 128], P('dp'), may hold values 0 or 1
- tile_live: int32 [1024], P('dp'), may hold values from 1 to 128
- tile_group: int32 [1024], P('dp'), may hold values from 0 to 127, as said below
- position: float32 [128, 2048], P('dp', 'feat'), may hold values from -2.4 to 2.4
- momentum: float32 [128, 2048], P('dp', 'feat'), may hold values from -6 to 6
- gradient: float32 [128, 2048], P('dp', 'feat'), may hold values from -18 to 18
- prior_mean: float32 [2048], P('feat'), may hold values from -1.8 to 1.8
- prior_prec: float32 [128], P('feat'), may hold values from 0.25 to 4
- inv_mass: float32 [128], P('feat'), may hold values from 0.5 to 2
Outputs:
- new_position: float32 [128, 2048], P('dp', 'feat')
- new_momentum: float32 [128, 2048], P('dp', 'feat')
- new_gradient: float32 [128, 2048], P('dp', 'feat')
- energy: float32 [128, 16], P('dp')
The draws below stay inside these ranges and needn't reach their ends.
Inputs may be any that keep to these rules, and one draw needn't show every extreme that they name: `tile_group`: group g belongs to owner g // 16. Among the 128 tiles of one device at most 32 have groups of any one owner, and one owner has exactly 32 tiles from every device. `tile_live`: the live slots of a tile come first.
All inputs are finite; a program needn't handle non-finite values. No bound on the sum of `labels` on one device may be relied on, other than what follows from the above.
Results may differ from the reference program's by a relative error of at most 0.0041.
Values may be sent and summed in bfloat16 or wider, within the bound.
No kernel may reach another device: no remote copies, remote signals or barrier semaphores. Data moves between devices by JAX's collectives and lax.ppermute only.
A program may use at most 64 MiB of HBM per device.

```python
import math
import jax
import jax.numpy as jnp
from jax import lax

F = 128
ROWS = 128
TILE_DEV = 128
GRP_DEV = 16
CHAINS = 16
NTILES = 1024
GROUPS = 128


def draw_tile_group(key, part):
    owners = GROUPS // GRP_DEV
    block_total = NTILES // TILE_DEV
    slot_count = max(2, 2 * TILE_DEV // owners)
    hot_owner = jax.random.randint(jax.random.fold_in(key, 11), (), 0, owners)
    spare_count = (owners - 1) * slot_count

    def one_block(block_index):
        block_key = jax.random.fold_in(jax.random.fold_in(key, 12), block_index)
        pick_key, order_key, local_key = jax.random.split(block_key, 3)
        candidate = jnp.arange(spare_count, dtype=jnp.int32) // slot_count
        candidate = candidate + (candidate >= hot_owner).astype(jnp.int32)
        chosen = jax.random.permutation(pick_key, candidate)[:TILE_DEV - slot_count]
        target = jnp.concatenate([jnp.full((slot_count,), hot_owner, jnp.int32), chosen.astype(jnp.int32)])
        target = jax.random.permutation(order_key, target)
        local_group = jax.random.randint(local_key, (TILE_DEV,), 0, GRP_DEV)
        return (target * GRP_DEV + local_group).astype(jnp.int32)
    return jax.vmap(one_block)(jnp.arange(block_total, dtype=jnp.int32)).reshape(NTILES).astype(jnp.int32)


def set_ends(drawn, rng, smallest, high):
    shape = drawn.shape
    index_at = [jax.random.randint(jax.random.fold_in(rng, axis), (), 0, shape[axis]) for axis in range(len(shape))]
    drawn = drawn.at[tuple(index_at)].set(smallest)
    longest = shape.index(max(shape))
    index_at[longest] = (index_at[longest] + 1) % shape[longest]
    return drawn.at[tuple(index_at)].set(high)


def block_levels(rng, dims, pieces, low, high):
    loudness = 1.0
    for dim, blocks in pieces:
        draws = jax.random.uniform(jax.random.fold_in(jax.random.fold_in(rng, 6), dim), (blocks,), jnp.float32, low / len(pieces), high / len(pieces))
        loudness = loudness * jnp.repeat(jnp.exp(draws), dims[dim] // blocks).reshape((-1,) + (1,) * (len(dims) - 1 - dim))
    return loudness


def noise(own_key, extent, width, most, pieces=(), kind=jnp.bfloat16):
    factor_of = block_levels(own_key, extent, pieces, -0.22, 0.18) if pieces else 1.0
    result = jax.random.normal(own_key, extent, jnp.float32) * width * factor_of
    return jnp.minimum(jnp.maximum(result, -most), most).astype(kind)


def setup_inputs(seed: int = 0) -> dict:
    arg_keys = jax.random.split(jax.random.key(seed), 11)
    observations = noise(arg_keys[0], (NTILES, F, ROWS), 0.25, 1.5, ((0, 8), (1, 4)))
    labels = set_ends((jax.random.randint(arg_keys[1], (NTILES, ROWS), 0, 2) < 1).astype(jnp.int32), jax.random.fold_in(arg_keys[1], 1), 0, 1)
    tile_live = set_ends(jax.random.randint(arg_keys[2], (NTILES,), 1, ROWS + 1), jax.random.fold_in(arg_keys[2], 1), 1, ROWS).astype(jnp.int32)
    tile_group = draw_tile_group(jax.random.fold_in(arg_keys[10], 71), 0)
    position = noise(arg_keys[4], (GROUPS, F * CHAINS), 0.4, 2.4, ((0, 8), (1, 4)), jnp.float32)
    momentum = noise(arg_keys[5], (GROUPS, F * CHAINS), 1.0, 6.0, ((0, 8), (1, 4)), jnp.float32)
    gradient = noise(arg_keys[6], (GROUPS, F * CHAINS), 3.0, 18.0, ((0, 8), (1, 4)), jnp.float32)
    prior_mean = noise(arg_keys[7], (F * CHAINS,), 0.3, 1.8, ((0, 4),), jnp.float32)
    prior_prec = jnp.clip(jnp.exp(math.log(4.0) - 2.7725887 * jax.random.uniform(arg_keys[8], (F,), jnp.float32) ** block_levels(arg_keys[8], (F,), ((0, 4),), -0.2, 0.2)), 0.25, 4.0)
    inv_mass = jnp.clip(jnp.exp(math.log(2.0) - 1.3862944 * jax.random.uniform(arg_keys[9], (F,), jnp.float32) ** block_levels(arg_keys[9], (F,), ((0, 4),), -0.2, 0.2)), 0.5, 2.0)
    return {"observations": observations, "labels": labels, "tile_live": tile_live, "tile_group": tile_group, "position": position, "momentum": momentum, "gradient": gradient, "prior_mean": prior_mean, "prior_prec": prior_prec, "inv_mass": inv_mass}


step_size = 0.1


def tile_terms(blocks, observations, labels, tile_live):
    logits = jnp.einsum("tfc,tfr->tcr", blocks.astype(jnp.float32), observations.astype(jnp.float32), precision=lax.Precision.HIGHEST)
    live_rows = (jnp.arange(observations.shape[2], dtype=jnp.int32)[None, :] < tile_live[:, None])[:, None, :]
    targets = labels.astype(jnp.float32)[:, None, :]
    residual = jnp.where(live_rows, jax.nn.sigmoid(logits) - targets, 0.0).astype(jnp.bfloat16)
    neg_loglik = jnp.sum(jnp.where(live_rows, jax.nn.softplus(logits) - targets * logits, 0.0), axis=2)
    partial_value = jnp.einsum("tfr,tcr->tfc", observations.astype(jnp.float32), residual.astype(jnp.float32), precision=lax.Precision.HIGHEST)
    return partial_value.reshape(partial_value.shape[0], -1), neg_loglik


def reference(observations, labels, tile_live, tile_group, position, momentum, gradient, prior_mean, prior_prec, inv_mass):
    prior_full = jnp.repeat(prior_prec, CHAINS)
    mass_full = jnp.repeat(inv_mass, CHAINS)
    half_momentum = momentum - 0.5 * step_size * gradient
    moved_position = position + step_size * mass_full * half_momentum
    rounded = moved_position.astype(jnp.bfloat16)
    block_total = NTILES // TILE_DEV

    def one_block(running, block_items):
        tile_obs, tile_labels, live_count, groups = block_items
        blocks = rounded[groups].reshape(groups.shape[0], F, CHAINS)
        partial_value, neg_loglik = tile_terms(blocks, tile_obs, tile_labels, live_count)
        return running, (partial_value, neg_loglik)

    block_items = (observations.reshape(block_total, TILE_DEV, F, ROWS), labels.reshape(block_total, TILE_DEV, ROWS), tile_live.reshape(block_total, TILE_DEV), tile_group.reshape(block_total, TILE_DEV))
    running, outputs = lax.scan(one_block, jnp.zeros((), jnp.float32), block_items)
    partials, losses = outputs
    likelihood_grad = jax.ops.segment_sum(partials.reshape(NTILES, F * CHAINS), tile_group, num_segments=GROUPS)
    group_loglik = jax.ops.segment_sum(losses.reshape(NTILES, CHAINS), tile_group, num_segments=GROUPS)
    offset = moved_position - prior_mean
    new_gradient = likelihood_grad + prior_full * offset
    new_momentum = half_momentum - 0.5 * step_size * new_gradient
    quadratic = 0.5 * (prior_full * offset * offset + mass_full * new_momentum * new_momentum)
    energy = group_loglik + jnp.sum(quadratic.reshape(GROUPS, F, CHAINS), axis=1)
    return moved_position, new_momentum, new_gradient, energy
```

```python
import jax
import jax.numpy as jnp
from jax import lax
from jax.sharding import PartitionSpec as P

step_size = 0.1


def likelihood(logits, labels, tile_live):
    row_count = logits.shape[2]
    live_rows = (jnp.arange(row_count, dtype=jnp.int32)[None, :] < tile_live[:, None])[:, None, :]
    targets = labels.astype(jnp.float32)[:, None, :]
    residual = jnp.where(live_rows, jax.nn.sigmoid(logits) - targets, 0.0).astype(jnp.bfloat16)
    neg_loglik = jnp.sum(
        jnp.where(live_rows, jax.nn.softplus(logits) - targets * logits, 0.0), axis=2
    )
    return (residual, neg_loglik)


def body(
    observations,
    labels,
    tile_live,
    tile_group,
    position,
    momentum,
    gradient,
    prior_mean,
    prior_prec,
    inv_mass,
):
    owners = lax.axis_size("dp")
    parts = lax.axis_size("feat")
    part_index = lax.axis_index("feat")
    tile_count, quarter, row_count = observations.shape
    own_groups, block_width = position.shape
    chains = block_width // quarter
    groups = owners * own_groups
    share = tile_count // parts

    share_obs = lax.all_to_all(
        observations.reshape(parts, share, quarter, row_count), "feat", 0, 0, tiled=True
    )

    prior_full = jnp.repeat(prior_prec, chains)
    mass_full = jnp.repeat(inv_mass, chains)
    half_momentum = momentum - 0.5 * step_size * gradient
    moved_position = position + step_size * mass_full * half_momentum
    rounded = moved_position.astype(jnp.bfloat16)
    table = lax.all_gather(rounded, ("feat", "dp"), axis=0, tiled=True)
    table = table.reshape(parts, groups, block_width)

    start = part_index * share
    share_labels = lax.dynamic_slice_in_dim(labels, start, share, 0)
    share_live = lax.dynamic_slice_in_dim(tile_live, start, share, 0)
    share_group = lax.dynamic_slice_in_dim(tile_group, start, share, 0)
    member = share_group[:, None] == jnp.arange(groups, dtype=jnp.int32)[None, :]

    coeffs = jnp.einsum(
        "tg,qgw->qtw", member.astype(jnp.bfloat16), table, preferred_element_type=jnp.float32
    ).astype(jnp.bfloat16)
    coeffs = coeffs.reshape(parts, share, quarter, chains)
    logits = jnp.einsum(
        "qtfc,qtfr->tcr", coeffs, share_obs, preferred_element_type=jnp.float32
    )
    residual, neg_loglik = likelihood(logits, share_labels, share_live)
    grad = jnp.einsum(
        "qtfr,tcr->tqfc", share_obs, residual, preferred_element_type=jnp.float32
    ).reshape(share, parts * block_width)
    chooser = member.astype(jnp.float32)
    group_grad = jnp.einsum(
        "tg,tw->gw", chooser, grad, precision=lax.Precision.HIGHEST,
        preferred_element_type=jnp.float32,
    ).astype(jnp.bfloat16)
    group_loglik = jnp.einsum(
        "tg,tc->gc", chooser, neg_loglik, precision=lax.Precision.HIGHEST,
        preferred_element_type=jnp.float32,
    )
    high = group_loglik.astype(jnp.bfloat16)
    low = (group_loglik - high.astype(jnp.float32)).astype(jnp.bfloat16)
    pad = jnp.zeros((groups, parts - 2, chains), jnp.bfloat16)
    tails = jnp.concatenate([high[:, None], low[:, None], pad], axis=1)
    send = jnp.concatenate([group_grad.reshape(groups, parts, block_width), tails], axis=2)
    send = send.reshape(owners, own_groups, parts, block_width + chains).transpose(0, 2, 1, 3)
    send = send.reshape(owners * parts, own_groups, block_width + chains)
    got = lax.all_to_all(send, ("dp", "feat"), 0, 0, tiled=True)
    summed = jnp.sum(got.astype(jnp.float32), axis=0)
    likelihood_grad = summed[:, :block_width]
    own_loglik = summed[:, block_width:]

    offset = moved_position - prior_mean
    new_gradient = likelihood_grad + prior_full * offset
    new_momentum = half_momentum - 0.5 * step_size * new_gradient
    quadratic = 0.5 * (prior_full * offset * offset + mass_full * new_momentum * new_momentum)
    quadratic = jnp.sum(quadratic.reshape(own_groups, quarter, chains), axis=1)
    energy = lax.psum(quadratic + own_loglik, "feat")
    return (moved_position, new_momentum, new_gradient, energy)


def solution(mesh):
    placed = (
        P("dp", "feat", None),
        P("dp", None),
        P("dp"),
        P("dp"),
        P("dp", "feat"),
        P("dp", "feat"),
        P("dp", "feat"),
        P("feat"),
        P("feat"),
        P("feat"),
    )
    return jax.shard_map(
        body,
        mesh=mesh,
        in_specs=placed,
        out_specs=(P("dp", "feat"), P("dp", "feat"), P("dp", "feat"), P("dp", None)),
        check_vma=False,
    )
```

```python
import jax
import jax.numpy as jnp
from jax import lax
from jax.sharding import PartitionSpec as P

step_size = 0.1


def likelihood(logits, labels, tile_live):
    row_count = logits.shape[2]
    live_rows = (jnp.arange(row_count, dtype=jnp.int32)[None, :] < tile_live[:, None])[:, None, :]
    targets = labels.astype(jnp.float32)[:, None, :]
    residual = jnp.where(live_rows, jax.nn.sigmoid(logits) - targets, 0.0).astype(jnp.bfloat16)
    neg_loglik = jnp.sum(
        jnp.where(live_rows, jax.nn.softplus(logits) - targets * logits, 0.0), axis=2
    )
    return (residual, neg_loglik)


def body(
    observations,
    labels,
    tile_live,
    tile_group,
    position,
    momentum,
    gradient,
    prior_mean,
    prior_prec,
    inv_mass,
):
    owners = lax.axis_size("dp")
    parts = lax.axis_size("feat")
    part_index = lax.axis_index("feat")
    tile_count, quarter, row_count = observations.shape
    own_groups, block_width = position.shape
    chains = block_width // quarter
    groups = owners * own_groups
    share = tile_count // parts

    share_obs = lax.all_to_all(
        observations.reshape(parts, share, quarter, row_count), "feat", 0, 0, tiled=True
    )

    prior_full = jnp.repeat(prior_prec, chains)
    mass_full = jnp.repeat(inv_mass, chains)
    half_momentum = momentum - 0.5 * step_size * gradient
    moved_position = position + step_size * mass_full * half_momentum
    rounded = moved_position.astype(jnp.bfloat16)
    copies = jnp.broadcast_to(rounded[None], (owners, own_groups, block_width))
    table = lax.all_to_all(copies, "dp", 0, 0, tiled=True).reshape(groups, block_width)
    table = lax.all_gather(table, "feat", axis=0, tiled=False)

    start = part_index * share
    share_labels = lax.dynamic_slice_in_dim(labels, start, share, 0)
    share_live = lax.dynamic_slice_in_dim(tile_live, start, share, 0)
    share_group = lax.dynamic_slice_in_dim(tile_group, start, share, 0)
    member = share_group[:, None] == jnp.arange(groups, dtype=jnp.int32)[None, :]

    coeffs = jnp.einsum(
        "tg,qgw->qtw", member.astype(jnp.bfloat16), table, preferred_element_type=jnp.float32
    ).astype(jnp.bfloat16)
    coeffs = coeffs.reshape(parts, share, quarter, chains)
    logits = jnp.einsum(
        "qtfc,qtfr->tcr", coeffs, share_obs, preferred_element_type=jnp.float32
    )
    residual, neg_loglik = likelihood(logits, share_labels, share_live)
    all_residual = lax.all_gather(residual, "feat", axis=0, tiled=True)
    grad = jnp.einsum(
        "tfr,tcr->tfc", observations, all_residual, preferred_element_type=jnp.float32
    ).reshape(tile_count, block_width)
    group_order = jnp.arange(groups, dtype=jnp.int32)
    chooser = (tile_group[:, None] == group_order[None, :]).astype(jnp.float32)
    group_grad = jnp.einsum(
        "tg,tw->gw", chooser, grad, precision=lax.Precision.HIGHEST,
        preferred_element_type=jnp.float32,
    ).astype(jnp.bfloat16)
    group_loglik = jnp.einsum(
        "tg,tc->gc", member.astype(jnp.float32), neg_loglik, precision=lax.Precision.HIGHEST,
        preferred_element_type=jnp.float32,
    )
    high = group_loglik.astype(jnp.bfloat16)
    low = (group_loglik - high.astype(jnp.float32)).astype(jnp.bfloat16)
    send = jnp.concatenate([group_grad, high, low], axis=1)
    send = send.reshape(owners, own_groups, block_width + 2 * chains)
    got = lax.all_to_all(send, "dp", 0, 0, tiled=True)
    summed = jnp.sum(got.astype(jnp.float32), axis=0)
    likelihood_grad = summed[:, :block_width]
    own_loglik = summed[:, block_width:block_width + chains] + summed[:, block_width + chains:]

    offset = moved_position - prior_mean
    new_gradient = likelihood_grad + prior_full * offset
    new_momentum = half_momentum - 0.5 * step_size * new_gradient
    quadratic = 0.5 * (prior_full * offset * offset + mass_full * new_momentum * new_momentum)
    quadratic = jnp.sum(quadratic.reshape(own_groups, quarter, chains), axis=1)
    energy = lax.psum(quadratic + own_loglik, "feat")
    return (moved_position, new_momentum, new_gradient, energy)


def solution(mesh):
    placed = (
        P("dp", "feat", None),
        P("dp", None),
        P("dp"),
        P("dp"),
        P("dp", "feat"),
        P("dp", "feat"),
        P("dp", "feat"),
        P("feat"),
        P("feat"),
        P("feat"),
    )
    return jax.shard_map(
        body,
        mesh=mesh,
        in_specs=placed,
        out_specs=(P("dp", "feat"), P("dp", "feat"), P("dp", "feat"), P("dp", None)),
        check_vma=False,
    )
```

```python
import jax
import jax.numpy as jnp
from jax import lax
from jax.sharding import PartitionSpec as P

step_size = 0.1


def likelihood(logits, labels, tile_live):
    row_count = logits.shape[2]
    live_rows = (jnp.arange(row_count, dtype=jnp.int32)[None, :] < tile_live[:, None])[:, None, :]
    targets = labels.astype(jnp.float32)[:, None, :]
    residual = jnp.where(live_rows, jax.nn.sigmoid(logits) - targets, 0.0).astype(jnp.bfloat16)
    neg_loglik = jnp.sum(
        jnp.where(live_rows, jax.nn.softplus(logits) - targets * logits, 0.0), axis=2
    )
    return (residual, neg_loglik)


def sum_over_feat(value):
    parts = lax.axis_size("feat")
    if parts & (parts - 1):
        return lax.psum(value, "feat")
    terms = [value] + [
        lax.ppermute(value, "feat", [(i, i ^ k) for i in range(parts)]) for k in range(1, parts)
    ]
    while len(terms) > 1:
        terms = [terms[i] + terms[i + 1] for i in range(0, len(terms), 2)]
    return terms[0]


def body(
    observations,
    labels,
    tile_live,
    tile_group,
    position,
    momentum,
    gradient,
    prior_mean,
    prior_prec,
    inv_mass,
):
    owners = lax.axis_size("dp")
    parts = lax.axis_size("feat")
    part_index = lax.axis_index("feat")
    tile_count, quarter, row_count = observations.shape
    own_groups, block_width = position.shape
    chains = block_width // quarter
    groups = owners * own_groups
    share = tile_count // parts

    prior_full = jnp.repeat(prior_prec, chains)
    mass_full = jnp.repeat(inv_mass, chains)
    half_momentum = momentum - 0.5 * step_size * gradient
    moved_position = position + step_size * mass_full * half_momentum
    rounded = moved_position.astype(jnp.bfloat16)
    copies = jnp.broadcast_to(rounded[None], (owners, own_groups, block_width))
    table = lax.all_to_all(copies, "dp", 0, 0, tiled=True).reshape(groups, block_width)

    start = part_index * share
    share_labels = lax.dynamic_slice_in_dim(labels, start, share, 0)
    share_live = lax.dynamic_slice_in_dim(tile_live, start, share, 0)
    share_group = lax.dynamic_slice_in_dim(tile_group, start, share, 0)
    member = share_group[:, None] == jnp.arange(groups, dtype=jnp.int32)[None, :]

    group_order = jnp.arange(groups, dtype=jnp.int32)
    belongs = tile_group[:, None] == group_order[None, :]
    coeffs = jnp.einsum(
        "tg,gw->tw", belongs.astype(jnp.bfloat16), table, preferred_element_type=jnp.float32
    ).astype(jnp.bfloat16)
    coeffs = coeffs.reshape(tile_count, quarter, chains)
    partial = jnp.einsum(
        "tfc,tfr->tcr", coeffs, observations, preferred_element_type=jnp.float32
    ).astype(jnp.bfloat16).reshape(parts, share, chains, row_count)
    logits = lax.dynamic_index_in_dim(partial, part_index, 0, False).astype(jnp.float32)
    for hop in range(1, parts):
        piece = lax.dynamic_index_in_dim(partial, (part_index + hop) % parts, 0, False)
        piece = lax.ppermute(piece, "feat", [(i, (i + hop) % parts) for i in range(parts)])
        logits = logits + piece.astype(jnp.float32)
    residual, neg_loglik = likelihood(logits, share_labels, share_live)
    all_residual = lax.all_gather(residual, "feat", axis=0, tiled=True)
    grad = jnp.einsum(
        "tfr,tcr->tfc", observations, all_residual, preferred_element_type=jnp.float32
    ).reshape(tile_count, block_width)
    chooser = belongs.astype(jnp.float32)
    group_grad = jnp.einsum(
        "tg,tw->gw", chooser, grad, precision=lax.Precision.HIGHEST,
        preferred_element_type=jnp.float32,
    ).astype(jnp.bfloat16)
    group_loglik = jnp.einsum(
        "tg,tc->gc", member.astype(jnp.float32), neg_loglik, precision=lax.Precision.HIGHEST,
        preferred_element_type=jnp.float32,
    )
    high = group_loglik.astype(jnp.bfloat16)
    low = (group_loglik - high.astype(jnp.float32)).astype(jnp.bfloat16)
    send = jnp.concatenate([group_grad, high, low], axis=1)
    send = send.reshape(owners, own_groups, block_width + 2 * chains)
    got = lax.all_to_all(send, "dp", 0, 0, tiled=True)
    summed = jnp.sum(got.astype(jnp.float32), axis=0)
    likelihood_grad = summed[:, :block_width]
    own_loglik = summed[:, block_width:block_width + chains] + summed[:, block_width + chains:]

    offset = moved_position - prior_mean
    new_gradient = likelihood_grad + prior_full * offset
    new_momentum = half_momentum - 0.5 * step_size * new_gradient
    quadratic = 0.5 * (prior_full * offset * offset + mass_full * new_momentum * new_momentum)
    quadratic = jnp.sum(quadratic.reshape(own_groups, quarter, chains), axis=1)
    energy = sum_over_feat(quadratic + own_loglik)
    return (moved_position, new_momentum, new_gradient, energy)


def solution(mesh):
    placed = (
        P("dp", "feat", None),
        P("dp", None),
        P("dp"),
        P("dp"),
        P("dp", "feat"),
        P("dp", "feat"),
        P("dp", "feat"),
        P("feat"),
        P("feat"),
        P("feat"),
    )
    return jax.shard_map(
        body,
        mesh=mesh,
        in_specs=placed,
        out_specs=(P("dp", "feat"), P("dp", "feat"), P("dp", "feat"), P("dp", None)),
        check_vma=False,
    )
```

```python
import jax
import jax.numpy as jnp
from jax import lax
from jax.experimental import pallas as pl
from jax.sharding import PartitionSpec as P

step_size = 0.1


def likelihood(logits, labels, tile_live):
    row_count = logits.shape[2]
    live_rows = (jnp.arange(row_count, dtype=jnp.int32)[None, :] < tile_live[:, None])[:, None, :]
    targets = labels.astype(jnp.float32)[:, None, :]
    residual = jnp.where(live_rows, jax.nn.sigmoid(logits) - targets, 0.0).astype(jnp.bfloat16)
    neg_loglik = jnp.sum(
        jnp.where(live_rows, jax.nn.softplus(logits) - targets * logits, 0.0), axis=2
    )
    return (residual, neg_loglik)


def sum_over_feat(value):
    parts = lax.axis_size("feat")
    if parts & (parts - 1):
        return lax.psum(value, "feat")
    terms = [value] + [
        lax.ppermute(value, "feat", [(i, i ^ k) for i in range(parts)]) for k in range(1, parts)
    ]
    while len(terms) > 1:
        terms = [terms[i] + terms[i + 1] for i in range(0, len(terms), 2)]
    return terms[0]


def opening(position, momentum, gradient, inv_mass, owners):
    own_groups, width = position.shape
    quarter = inv_mass.shape[0]
    chains = width // quarter

    def kernel(mass_ref, position_ref, momentum_ref, gradient_ref, half_ref, moved_ref, copies_ref):
        feature = lax.broadcasted_iota(jnp.int32, (quarter, width), 0)
        entry = lax.broadcasted_iota(jnp.int32, (quarter, width), 1)
        first = feature * chains
        spread = ((entry >= first) & (entry < first + chains)).astype(jnp.float32)
        mass = jnp.dot(
            mass_ref[...], spread, precision=lax.Precision.HIGHEST,
            preferred_element_type=jnp.float32,
        )
        half = momentum_ref[...] - 0.5 * step_size * gradient_ref[...]
        moved = position_ref[...] + step_size * mass * half
        half_ref[...] = half
        moved_ref[...] = moved
        rounded = moved.astype(jnp.bfloat16)
        for owner in range(copies_ref.shape[0]):
            copies_ref[owner] = rounded

    return pl.pallas_call(
        kernel,
        out_shape=(
            jax.ShapeDtypeStruct((own_groups, width), jnp.float32),
            jax.ShapeDtypeStruct((own_groups, width), jnp.float32),
            jax.ShapeDtypeStruct((owners, own_groups, width), jnp.bfloat16),
        ),
        name="opening",
    )(inv_mass[None], position, momentum, gradient)


def body(
    observations,
    labels,
    tile_live,
    tile_group,
    position,
    momentum,
    gradient,
    prior_mean,
    prior_prec,
    inv_mass,
):
    owners = lax.axis_size("dp")
    parts = lax.axis_size("feat")
    part_index = lax.axis_index("feat")
    tile_count, quarter, row_count = observations.shape
    own_groups, block_width = position.shape
    chains = block_width // quarter
    groups = owners * own_groups
    share = tile_count // parts

    prior_full = jnp.repeat(prior_prec, chains)
    mass_full = jnp.repeat(inv_mass, chains)
    half_momentum, moved_position, copies = opening(
        position, momentum, gradient, inv_mass, owners
    )
    table = lax.all_to_all(copies, "dp", 0, 0, tiled=True).reshape(groups, block_width)

    start = part_index * share
    share_labels = lax.dynamic_slice_in_dim(labels, start, share, 0)
    share_live = lax.dynamic_slice_in_dim(tile_live, start, share, 0)
    share_group = lax.dynamic_slice_in_dim(tile_group, start, share, 0)
    member = share_group[:, None] == jnp.arange(groups, dtype=jnp.int32)[None, :]

    group_order = jnp.arange(groups, dtype=jnp.int32)
    belongs = tile_group[:, None] == group_order[None, :]
    coeffs = jnp.einsum(
        "tg,gw->tw", belongs.astype(jnp.bfloat16), table, preferred_element_type=jnp.float32
    ).astype(jnp.bfloat16)
    coeffs = coeffs.reshape(tile_count, quarter, chains)
    partial = jnp.einsum(
        "tfc,tfr->tcr", coeffs, observations, preferred_element_type=jnp.float32
    ).astype(jnp.bfloat16).reshape(parts, share, chains, row_count)
    logits = lax.dynamic_index_in_dim(partial, part_index, 0, False).astype(jnp.float32)
    for hop in range(1, parts):
        piece = lax.dynamic_index_in_dim(partial, (part_index + hop) % parts, 0, False)
        piece = lax.ppermute(piece, "feat", [(i, (i + hop) % parts) for i in range(parts)])
        logits = logits + piece.astype(jnp.float32)
    residual, neg_loglik = likelihood(logits, share_labels, share_live)
    all_residual = lax.all_gather(residual, "feat", axis=0, tiled=True)
    grad = jnp.einsum(
        "tfr,tcr->tfc", observations, all_residual, preferred_element_type=jnp.float32
    ).reshape(tile_count, block_width)
    chooser = belongs.astype(jnp.float32)
    group_grad = jnp.einsum(
        "tg,tw->gw", chooser, grad, precision=lax.Precision.HIGHEST,
        preferred_element_type=jnp.float32,
    ).astype(jnp.bfloat16)
    group_loglik = jnp.einsum(
        "tg,tc->gc", member.astype(jnp.float32), neg_loglik, precision=lax.Precision.HIGHEST,
        preferred_element_type=jnp.float32,
    )
    high = group_loglik.astype(jnp.bfloat16)
    low = (group_loglik - high.astype(jnp.float32)).astype(jnp.bfloat16)
    send = jnp.concatenate([group_grad, high, low], axis=1)
    send = send.reshape(owners, own_groups, block_width + 2 * chains)
    got = lax.all_to_all(send, "dp", 0, 0, tiled=True)
    summed = jnp.sum(got.astype(jnp.float32), axis=0)
    likelihood_grad = summed[:, :block_width]
    own_loglik = summed[:, block_width:block_width + chains] + summed[:, block_width + chains:]

    offset = moved_position - prior_mean
    new_gradient = likelihood_grad + prior_full * offset
    new_momentum = half_momentum - 0.5 * step_size * new_gradient
    quadratic = 0.5 * (prior_full * offset * offset + mass_full * new_momentum * new_momentum)
    quadratic = jnp.sum(quadratic.reshape(own_groups, quarter, chains), axis=1)
    energy = sum_over_feat(quadratic + own_loglik)
    return (moved_position, new_momentum, new_gradient, energy)


def solution(mesh):
    placed = (
        P("dp", "feat", None),
        P("dp", None),
        P("dp"),
        P("dp"),
        P("dp", "feat"),
        P("dp", "feat"),
        P("dp", "feat"),
        P("feat"),
        P("feat"),
        P("feat"),
    )
    return jax.shard_map(
        body,
        mesh=mesh,
        in_specs=placed,
        out_specs=(P("dp", "feat"), P("dp", "feat"), P("dp", "feat"), P("dp", None)),
        check_vma=False,
    )
```

```python
import jax
import jax.numpy as jnp
from jax import lax
from jax.experimental import pallas as pl
from jax.sharding import PartitionSpec as P

step_size = 0.1


def likelihood(logits, labels, tile_live):
    row_count = logits.shape[2]
    live_rows = (jnp.arange(row_count, dtype=jnp.int32)[None, :] < tile_live[:, None])[:, None, :]
    targets = labels.astype(jnp.float32)[:, None, :]
    residual = jnp.where(live_rows, jax.nn.sigmoid(logits) - targets, 0.0).astype(jnp.bfloat16)
    neg_loglik = jnp.sum(
        jnp.where(live_rows, jax.nn.softplus(logits) - targets * logits, 0.0), axis=2
    )
    return (residual, neg_loglik)


def sum_over_feat(value):
    parts = lax.axis_size("feat")
    if parts & (parts - 1):
        return lax.psum(value, "feat")
    terms = [value] + [
        lax.ppermute(value, "feat", [(i, i ^ k) for i in range(parts)]) for k in range(1, parts)
    ]
    while len(terms) > 1:
        terms = [terms[i] + terms[i + 1] for i in range(0, len(terms), 2)]
    return terms[0]


def opening(position, momentum, gradient, inv_mass, owners):
    own_groups, width = position.shape
    quarter = inv_mass.shape[0]
    chains = width // quarter

    def kernel(mass_ref, position_ref, momentum_ref, gradient_ref, half_ref, moved_ref, copies_ref):
        feature = lax.broadcasted_iota(jnp.int32, (quarter, width), 0)
        entry = lax.broadcasted_iota(jnp.int32, (quarter, width), 1)
        first = feature * chains
        spread = ((entry >= first) & (entry < first + chains)).astype(jnp.float32)
        mass = jnp.dot(
            mass_ref[...], spread, precision=lax.Precision.HIGHEST,
            preferred_element_type=jnp.float32,
        )
        half = momentum_ref[...] - 0.5 * step_size * gradient_ref[...]
        moved = position_ref[...] + step_size * mass * half
        half_ref[...] = half
        moved_ref[...] = moved
        rounded = moved.astype(jnp.bfloat16)
        for owner in range(copies_ref.shape[0]):
            copies_ref[owner] = rounded

    return pl.pallas_call(
        kernel,
        out_shape=(
            jax.ShapeDtypeStruct((own_groups, width), jnp.float32),
            jax.ShapeDtypeStruct((own_groups, width), jnp.float32),
            jax.ShapeDtypeStruct((owners, own_groups, width), jnp.bfloat16),
        ),
        name="opening",
    )(inv_mass[None], position, momentum, gradient)


def body(
    observations,
    labels,
    tile_live,
    tile_group,
    position,
    momentum,
    gradient,
    prior_mean,
    prior_prec,
    inv_mass,
):
    owners = lax.axis_size("dp")
    parts = lax.axis_size("feat")
    part_index = lax.axis_index("feat")
    tile_count, quarter, row_count = observations.shape
    own_groups, block_width = position.shape
    chains = block_width // quarter
    groups = owners * own_groups
    share = tile_count // parts

    prior_full = jnp.repeat(prior_prec, chains)
    mass_full = jnp.repeat(inv_mass, chains)
    half_momentum, moved_position, copies = opening(
        position, momentum, gradient, inv_mass, owners
    )
    table = lax.all_to_all(copies, "dp", 0, 0, tiled=True).reshape(groups, block_width)

    start = part_index * share
    share_labels = lax.dynamic_slice_in_dim(labels, start, share, 0)
    share_live = lax.dynamic_slice_in_dim(tile_live, start, share, 0)
    share_group = lax.dynamic_slice_in_dim(tile_group, start, share, 0)
    member = share_group[:, None] == jnp.arange(groups, dtype=jnp.int32)[None, :]

    group_order = jnp.arange(groups, dtype=jnp.int32)
    belongs = tile_group[:, None] == group_order[None, :]
    coeffs = jnp.einsum(
        "tg,gw->tw", belongs.astype(jnp.bfloat16), table, preferred_element_type=jnp.float32
    ).astype(jnp.bfloat16)
    coeffs = coeffs.reshape(tile_count, quarter, chains)
    partial = jnp.einsum(
        "tfc,tfr->tcr", coeffs, observations, preferred_element_type=jnp.float32
    ).astype(jnp.bfloat16).reshape(parts, share, chains, row_count)
    logits = lax.dynamic_index_in_dim(partial, part_index, 0, False).astype(jnp.float32)
    for hop in range(1, parts):
        piece = lax.dynamic_index_in_dim(partial, (part_index + hop) % parts, 0, False)
        piece = lax.ppermute(piece, "feat", [(i, (i + hop) % parts) for i in range(parts)])
        logits = logits + piece.astype(jnp.float32)
    residual, neg_loglik = likelihood(logits, share_labels, share_live)
    all_residual = lax.all_gather(residual, "feat", axis=0, tiled=True)
    grad = jnp.einsum(
        "tfr,tcr->tfc", observations, all_residual, preferred_element_type=jnp.float32
    ).reshape(tile_count, block_width)
    chooser = belongs.astype(jnp.float32)
    group_grad = jnp.einsum(
        "tg,tw->gw", chooser, grad, precision=lax.Precision.HIGHEST,
        preferred_element_type=jnp.float32,
    ).astype(jnp.bfloat16)
    group_loglik = jnp.einsum(
        "tg,tc->gc", member.astype(jnp.float32), neg_loglik, precision=lax.Precision.HIGHEST,
        preferred_element_type=jnp.float32,
    )
    high = group_loglik.astype(jnp.bfloat16)
    low = (group_loglik - high.astype(jnp.float32)).astype(jnp.bfloat16)
    send = jnp.concatenate([group_grad, high, low], axis=1)
    send = send.reshape(owners, own_groups, block_width + 2 * chains)
    if owners & (owners - 1) or owners > 2 * parts:
        got = lax.all_to_all(send, "dp", 0, 0, tiled=True)
        summed = jnp.sum(got.astype(jnp.float32), axis=0)
    else:
        me = lax.axis_index("dp")
        halves = send.reshape(owners // 2, 2, own_groups, block_width + 2 * chains)
        theirs = lax.dynamic_index_in_dim(halves, (me % 2) ^ 1, 1, False)
        theirs = lax.ppermute(theirs, "dp", [(i, i ^ 1) for i in range(owners)])
        kept = lax.dynamic_index_in_dim(halves, me % 2, 1, False).astype(jnp.float32)
        kept = kept + theirs.astype(jnp.float32)
        level = me // 2
        summed = lax.dynamic_index_in_dim(kept, level, 0, False)
        for k in range(1, owners // 2):
            piece = lax.dynamic_index_in_dim(kept, level ^ k, 0, False)
            piece = lax.ppermute(piece, "dp", [(i, i ^ (2 * k)) for i in range(owners)])
            summed = summed + piece
    likelihood_grad = summed[:, :block_width]
    own_loglik = summed[:, block_width:block_width + chains] + summed[:, block_width + chains:]

    offset = moved_position - prior_mean
    new_gradient = likelihood_grad + prior_full * offset
    new_momentum = half_momentum - 0.5 * step_size * new_gradient
    quadratic = 0.5 * (prior_full * offset * offset + mass_full * new_momentum * new_momentum)
    quadratic = jnp.sum(quadratic.reshape(own_groups, quarter, chains), axis=1)
    energy = sum_over_feat(quadratic + own_loglik)
    return (moved_position, new_momentum, new_gradient, energy)


def solution(mesh):
    placed = (
        P("dp", "feat", None),
        P("dp", None),
        P("dp"),
        P("dp"),
        P("dp", "feat"),
        P("dp", "feat"),
        P("dp", "feat"),
        P("feat"),
        P("feat"),
        P("feat"),
    )
    return jax.shard_map(
        body,
        mesh=mesh,
        in_specs=placed,
        out_specs=(P("dp", "feat"), P("dp", "feat"), P("dp", "feat"), P("dp", None)),
        check_vma=False,
    )
```
